32 devices in a mesh: shards: 4 (over y, core), context: 2 (over x), tensor: 4 (over z).
Axes of the slice: x: 2, y: 2, z: 4, core: 2. Of those that a mesh axis runs over, the one named last changes fastest.
Arguments:
- frames_in: bfloat16 [4, 1500, 768], P('shards', 'context'), may hold values from -6 to 6
- grad_out: bfloat16 [4, 1500, 768], P('shards', 'context'), may hold values from -6 to 6
- norm_gains: bfloat16 [2, 768], P(None, 'shards'), may hold values from 0.5 to 1.5
- vec_biases: bfloat16 [4, 768], P(None, 'shards'), may hold values from -3 to 3
- w_qkv: bfloat16 [768, 3, 768], P('shards', None, 'tensor'), may hold values from -1 to 1
- b_qv: bfloat16 [2, 12, 64], P(None, 'tensor', 'shards'), may hold values from -3 to 3
- w_out: bfloat16 [768, 768], P('tensor', 'shards'), may hold values from -0.4375 to 0.4375
- w_up: bfloat16 [768, 3072], P('shards', 'tensor'), may hold values from -0.21875 to 0.21875
- b_up: bfloat16 [48, 64], P('tensor', 'shards'), may hold values from -3 to 3
- w_down: bfloat16 [3072, 768], P('tensor', 'shards'), may hold values from -0.109375 to 0.109375
Outputs:
- block_out: float32 [4, 1500, 768], P('shards', 'context')
- grad_in: float32 [4, 1500, 768], P('shards', 'context')
- grad_norm_gains: float32 [2, 768], P(None, 'shards')
- grad_vec_biases: float32 [4, 768], P(None, 'shards')
- grad_w_qkv: float32 [768, 3, 768], P('shards', None, 'tensor')
- grad_b_qv: float32 [2, 12, 64], P(None, 'tensor', 'shards')
- grad_w_out: float32 [768, 768], P('tensor', 'shards')
- grad_w_up: float32 [768, 3072], P('shards', 'tensor')
- grad_b_up: float32 [48, 64], P('tensor', 'shards')
- grad_w_down: float32 [3072, 768], P('tensor', 'shards')
The draws below stay inside these ranges and needn't reach their ends.
All inputs are finite; a program needn't handle non-finite values.
Results may differ from the reference program's by a relative error of at most 0.014.
Values may be sent and summed in bfloat16 or wider, within the bound.
No kernel may reach another device: no remote copies, remote signals or barrier semaphores. Data moves between devices by JAX's collectives and lax.ppermute only.
A program may use at most 128 MiB of HBM per device.

```python
import jax
import jax.numpy as jnp
from jax import lax

D = 768
HEADS = 12
HD = 64
FF = 3072
LEN = 1500
CLIPS = 4


def draw_w_qkv(key, part):
    normal = jax.random.normal(jax.random.fold_in(key, 11), (D, 3, D), jnp.float32)
    weights = jnp.clip(normal, -5.0, 5.0) * D ** (-0.5)
    return jnp.clip(weights, -1.0, 1.0).astype(jnp.bfloat16)


def strengthened(drawn, rng, source, target, blocks, factor):
    def block_of(dim):
        return (jnp.arange(drawn.shape[dim]) // (drawn.shape[dim] // blocks)).reshape((-1,) + (1,) * (drawn.ndim - 1 - dim))

    first = jax.random.permutation(rng, blocks)[block_of(target)]
    second = (block_of(target) + blocks // 2) % blocks
    return jnp.where((block_of(source) == first) | (block_of(source) == second), factor * drawn, drawn)


def block_scale(stream_key, shape, split, low, high):
    loudness, own = 1.0, jax.random.fold_in(stream_key, 6)
    for dim, blocks in split:
        steps = jnp.exp(jax.random.uniform(jax.random.fold_in(own, dim), (blocks,), jnp.float32, low / len(split), high / len(split)))
        loudness = loudness * jnp.repeat(steps, shape[dim] // blocks).reshape([-1 if axis == dim else 1 for axis in range(len(shape))])
    return loudness


def noise(stream_key, dims, width, reach, split=(), kind=jnp.bfloat16):
    gain = block_scale(stream_key, dims, split, -0.22, 0.18) if split else 1.0
    array = jax.random.normal(stream_key, dims, jnp.float32) * width * gain
    return jnp.minimum(jnp.maximum(array, -reach), reach).astype(kind)


def bell_draw_with(key, extent, deviation, limit, split, heavy, held_as=jnp.bfloat16):
    result = deviation * jax.random.normal(key, extent, jnp.float32)
    if split:
        result = result * block_scale(key, extent, split, -0.22, 0.18)
    return jnp.clip(strengthened(result, jax.random.fold_in(key, 3), *heavy), -limit, limit).astype(held_as)


def setup_inputs(seed: int = 0) -> dict:
    seeds = jax.random.split(jax.random.key(seed), 11)
    return {
        "frames_in": noise(seeds[0], (CLIPS, LEN, D), 1.0, 6.0, ((0, 4), (1, 2))),
        "grad_out": bell_draw_with(seeds[1], (CLIPS, LEN, D), 1.0, 6.0, ((0, 4), (1, 2)), (0, 2, 4, 2.0)),
        "norm_gains": jnp.clip(1.0 + 0.1 * jax.random.normal(seeds[2], (2, D), jnp.float32), 0.5, 1.5).astype(jnp.bfloat16),
        "vec_biases": noise(seeds[3], (4, D), 0.5, 3.0, ((1, 4),)),
        "w_qkv": draw_w_qkv(jax.random.fold_in(seeds[10], 71), 0),
        "b_qv": noise(seeds[5], (2, HEADS, HD), 0.5, 3.0, ((1, 4), (2, 4))),
        "w_out": noise(seeds[6], (D, D), (D // 4) ** -0.5, 0.4375, ((0, 4), (1, 4))),
        "w_up": noise(seeds[7], (D, FF), D ** -0.5, 0.21875, ((0, 4), (1, 4))),
        "b_up": noise(seeds[8], (FF // HD, HD), 0.5, 3.0, ((0, 4), (1, 4))),
        "w_down": noise(seeds[9], (FF, D), FF ** -0.5, 0.109375, ((0, 4), (1, 4))),
    }


NORM_EPS = 1e-05
ROOT_HALF = 0.7071067811865476

@jax.custom_vjp
def low(v):
    return lax.optimization_barrier(v.astype(jnp.bfloat16)).astype(jnp.float32)

@jax.custom_vjp
def low_back(v):
    return v

def low_keep(v):
    return (low(v), None)

def low_pass(kept, grad):
    return (grad,)

def back_keep(v):
    return (v, None)

def back_low(kept, grad):
    return (low(grad),)
low.defvjp(low_keep, low_pass)
low_back.defvjp(back_keep, back_low)

def layer_norm(rows_in, gain_vec, shift_vec):
    row_mean = lax.optimization_barrier(jnp.mean(rows_in, axis=-1, keepdims=True))
    centred = rows_in - row_mean
    variance = lax.optimization_barrier(jnp.mean(centred * centred, axis=-1, keepdims=True))
    return centred * lax.rsqrt(variance + NORM_EPS) * gain_vec + shift_vec

def gelu_exact(pre_act):
    return 0.5 * pre_act * (1.0 + lax.erf(pre_act * ROOT_HALF))

def matmul_high(left_op, right_op):
    return jnp.dot(left_op, right_op, precision=lax.Precision.HIGHEST, preferred_element_type=jnp.float32)

def forward_clip(frames, params):
    gains, biases, qkv_weight, qkv_bias, out_weight, up_weight, up_bias, down_weight = params
    act_one = low(layer_norm(frames, gains[0], biases[0]))
    products = matmul_high(act_one, qkv_weight.reshape(D, 3 * D)).reshape(LEN, 3, D)
    bias_flat = qkv_bias.reshape(2, D)
    queries = low(low_back(products[:, 0]) + bias_flat[0])
    key_rows = low(low_back(products[:, 1]))
    value_rows = low(low_back(products[:, 2]) + bias_flat[1])
    query_heads = queries.reshape(LEN, HEADS, HD)
    key_heads = key_rows.reshape(LEN, HEADS, HD)
    value_heads = value_rows.reshape(LEN, HEADS, HD)
    scores = low_back(HD ** (-0.5) * jnp.einsum('qhd,khd->hqk', query_heads, key_heads, precision=lax.Precision.HIGHEST))
    attn_probs = jax.nn.softmax(scores, axis=-1)
    mixed = jnp.einsum('hqk,khd->qhd', low(attn_probs), value_heads, precision=lax.Precision.HIGHEST).reshape(LEN, D)
    mixed_low = low(low_back(mixed))
    residual = frames + (low_back(matmul_high(mixed_low, out_weight)) + biases[1])
    act_two = low(layer_norm(residual, gains[1], biases[2]))
    upper_sum = low_back(matmul_high(act_two, up_weight)) + up_bias.reshape(FF)
    hidden_low = low(gelu_exact(upper_sum))
    return residual + (low_back(matmul_high(hidden_low, down_weight)) + biases[3])

def reference(frames_in, grad_out, norm_gains, vec_biases, w_qkv, b_qv, w_out, w_up, b_up, w_down):
    params = (norm_gains.astype(jnp.float32), vec_biases.astype(jnp.float32), w_qkv.astype(jnp.float32), b_qv.astype(jnp.float32), w_out.astype(jnp.float32), w_up.astype(jnp.float32), b_up.astype(jnp.float32), w_down.astype(jnp.float32))

    def clip_step(totals, clip_pair):
        clip_frames, clip_cotan = clip_pair
        block, back_fn = jax.vjp(forward_clip, clip_frames, params)
        grad_frames, grad_params = back_fn(clip_cotan)
        totals = jax.tree.map(lambda total_in, extra_in: total_in + extra_in, totals, grad_params)
        return (totals, (block, grad_frames))
    zero_grads = jax.tree.map(jnp.zeros_like, params)
    totals, outputs = lax.scan(clip_step, zero_grads, (frames_in.astype(jnp.float32), grad_out.astype(jnp.float32)))
    block_out, grad_in = outputs
    return (block_out, grad_in, totals[0], totals[1], totals[2], totals[3], totals[4], totals[5], totals[6], totals[7])
```

```python
from functools import partial

import jax
import jax.numpy as jnp
from jax import lax
from jax.experimental import pallas as pl
from jax.experimental.pallas import tpu as pltpu
from jax.sharding import PartitionSpec as P

NORM_EPS = 1e-05
ROOT_HALF = 0.7071067811865476
INV_ROOT_2PI = 0.3989422804014327
BF = jnp.bfloat16
F32 = jnp.float32
QB = 256


def dot(a, b, ca, cb):
    return lax.dot_general(a, b, (((ca,), (cb,)), ((), ())), preferred_element_type=F32)


def norm_stats(v):
    mean = jnp.mean(v, axis=-1, keepdims=True)
    cen = v - mean
    rstd = lax.rsqrt(jnp.mean(cen * cen, axis=-1, keepdims=True) + NORM_EPS)
    return cen * rstd, rstd


def norm_back(dn, gain, xh, rstd):
    dxh = dn * gain
    return rstd * (
        dxh
        - jnp.mean(dxh, axis=-1, keepdims=True)
        - xh * jnp.mean(dxh * xh, axis=-1, keepdims=True)
    )


def key_bias(rows, frames):
    idx = lax.broadcasted_iota(jnp.int32, (rows, 1), 0)
    return jnp.where(idx < frames, 0.0, -1e30).astype(F32)


def attn_fwd_kernel(heads, hd, frames, scale, q_ref, *refs):
    n = len(heads)
    kv = refs[: 2 * n]
    o_ref, lse_ref = refs[2 * n :]
    rows = kv[0].shape[0]
    kb = key_bias(rows, frames)
    outs = []
    for i, h in enumerate(heads):
        q = (q_ref[:, h * hd : (h + 1) * hd].astype(F32) * scale).astype(BF)
        own, oth = kv[2 * i], kv[2 * i + 1]
        s0 = dot(own[:, :hd], q, 1, 1) + kb
        s1 = dot(oth[:, :hd], q, 1, 1) + kb
        m = jnp.maximum(jnp.max(s0, axis=0, keepdims=True), jnp.max(s1, axis=0, keepdims=True))
        e0 = jnp.exp(s0 - m)
        e1 = jnp.exp(s1 - m)
        tot = jnp.sum(e0, axis=0, keepdims=True) + jnp.sum(e1, axis=0, keepdims=True)
        ot = dot(own[:, hd:], e0.astype(BF), 0, 0) + dot(oth[:, hd:], e1.astype(BF), 0, 0)
        outs.append((ot * (1.0 / tot)).T.astype(BF))
        lse_ref[i : i + 1, :] = m + jnp.log(tot)
    o_ref[...] = outs[0] if n == 1 else jnp.concatenate(outs, axis=1)


def attn_fwd(q, kvs, heads, hd, frames, scale):
    rows, width = q.shape
    n = len(heads)
    ops = []
    for own, oth in kvs:
        ops += [own, oth]
    full = pl.BlockSpec((rows, 2 * hd), lambda i: (0, 0))
    return pl.pallas_call(
        partial(attn_fwd_kernel, heads, hd, frames, scale),
        grid=(rows // QB,),
        in_specs=[pl.BlockSpec((QB, width), lambda i: (i, 0))] + [full] * (2 * n),
        out_specs=[
            pl.BlockSpec((QB, n * hd), lambda i: (i, 0)),
            pl.BlockSpec((n, QB), lambda i: (0, i)),
        ],
        out_shape=[
            jax.ShapeDtypeStruct((rows, n * hd), BF),
            jax.ShapeDtypeStruct((n, rows), F32),
        ],
        compiler_params=pltpu.CompilerParams(vmem_limit_bytes=50 * 1024 * 1024),
        name="attn_fwd%d" % heads[0],
    )(q, *ops)


def attn_bwd_kernel(h, hd, frames, scale, q_ref, own_ref, oth_ref, lse_ref, g_ref, dq_ref, down_ref, doth_ref, acc0, acc1):
    i = pl.program_id(0)
    rows = own_ref.shape[0]
    kb = key_bias(rows, frames)
    q = (q_ref[:, h * hd : (h + 1) * hd].astype(F32) * scale).astype(BF)
    g = g_ref[:, h * hd : (h + 1) * hd]
    lse = lse_ref[...]
    p0 = jnp.exp(dot(own_ref[:, :hd], q, 1, 1) + (kb - lse))
    p1 = jnp.exp(dot(oth_ref[:, :hd], q, 1, 1) + (kb - lse))
    d0 = dot(own_ref[:, hd:], g, 1, 1)
    d1 = dot(oth_ref[:, hd:], g, 1, 1)
    inner = jnp.sum(p0 * d0, axis=0, keepdims=True) + jnp.sum(p1 * d1, axis=0, keepdims=True)
    ds0 = (p0 * (d0 - inner)).astype(BF)
    ds1 = (p1 * (d1 - inner)).astype(BF)
    c0 = jnp.concatenate([dot(ds0, q, 1, 0), dot(p0.astype(BF), g, 1, 0)], axis=1)
    c1 = jnp.concatenate([dot(ds1, q, 1, 0), dot(p1.astype(BF), g, 1, 0)], axis=1)
    dqt = dot(own_ref[:, :hd], ds0, 0, 0) + dot(oth_ref[:, :hd], ds1, 0, 0)
    dq_ref[...] = (dqt * scale).T

    @pl.when(i == 0)
    def _():
        acc0[...] = c0
        acc1[...] = c1

    @pl.when(i > 0)
    def _():
        acc0[...] += c0
        acc1[...] += c1

    @pl.when(i == pl.num_programs(0) - 1)
    def _():
        down_ref[...] = acc0[...]
        doth_ref[...] = acc1[...].astype(BF)


def attn_bwd(q, own, oth, lse, gob, h, hd, frames, scale):
    rows, width = q.shape
    full = pl.BlockSpec((rows, 2 * hd), lambda i: (0, 0))
    return pl.pallas_call(
        partial(attn_bwd_kernel, h, hd, frames, scale),
        grid=(rows // QB,),
        in_specs=[
            pl.BlockSpec((QB, width), lambda i: (i, 0)),
            full,
            full,
            pl.BlockSpec((1, QB), lambda i: (0, i)),
            pl.BlockSpec((QB, width), lambda i: (i, 0)),
        ],
        out_specs=[pl.BlockSpec((QB, hd), lambda i: (i, 0)), full, full],
        out_shape=[
            jax.ShapeDtypeStruct((rows, hd), F32),
            jax.ShapeDtypeStruct((rows, 2 * hd), F32),
            jax.ShapeDtypeStruct((rows, 2 * hd), BF),
        ],
        scratch_shapes=[pltpu.VMEM((rows, 2 * hd), F32), pltpu.VMEM((rows, 2 * hd), F32)],
        compiler_params=pltpu.CompilerParams(vmem_limit_bytes=50 * 1024 * 1024),
        name="attn_bwd%d" % h,
    )(q, own, oth, lse, gob)


def per_device(frames_in, grad_out, norm_gains, vec_biases, w_qkv, b_qv, w_out, w_up, b_up, w_down):
    clip_count, frames, D = frames_in.shape
    n_sh, n_t = lax.axis_size("shards"), lax.axis_size("tensor")
    assert clip_count == 1 and n_t == 4 and lax.axis_size("context") == 2
    bits = [b for b in range(n_sh.bit_length() - 1)]
    heads = b_qv.shape[1]
    hd = b_qv.shape[2] * n_sh
    pw = w_qkv.shape[2]
    hid = w_up.shape[1]
    dsh = w_qkv.shape[0]
    scale = hd ** (-0.5)
    CH = -(-frames // (4 * 64)) * 64
    R = 4 * CH

    s, c, z = lax.axis_index("shards"), lax.axis_index("context"), lax.axis_index("tensor")
    k, hi = s % 2, s // 2
    a, p = z // 2, z % 2
    o = 2 * k + p

    def perm_s(x, f):
        return lax.ppermute(x, "shards", [(i, f(i)) for i in range(n_sh)])

    def perm_z(x, f):
        return lax.ppermute(x, "tensor", [(i, f(i)) for i in range(n_t)])

    def perm_x(x):
        return lax.ppermute(x, "context", [(0, 1), (1, 0)])

    def perm_sz(x, f):
        pairs = []
        for i in range(n_sh):
            for j in range(n_t):
                t = f(i, j)
                if t is not None:
                    pairs.append((i * n_t + j, t[0] * n_t + t[1]))
        return lax.ppermute(x, ("shards", "tensor"), pairs)

    def dyn(x, i, axis=0):
        return lax.dynamic_index_in_dim(x, i, axis, keepdims=False)

    def core_swap(x):
        return perm_s(x, lambda i: i ^ 1)

    wk, wv, wq = w_qkv[:, 1], w_qkv[:, 2], w_qkv[:, 0]
    cols = []
    for h in range(heads):
        cols += [wk[:, h * hd : (h + 1) * hd], wv[:, h * hd : (h + 1) * hd]]
    cols.append(wq)
    shard_qkv = jnp.concatenate(cols, axis=1)
    small = jnp.concatenate([norm_gains, vec_biases], axis=0)
    small = jnp.pad(small, ((0, 0), (0, 3 * pw - dsh)))
    bq_flat = jnp.pad(b_qv.reshape(1, -1), ((0, 0), (0, 3 * pw - b_qv.size)))
    pack = jnp.concatenate([shard_qkv, small, bq_flat, jnp.zeros((1, 3 * pw), BF)], axis=0)
    allp = lax.all_gather(pack, "shards", axis=0, tiled=False)
    w_all = allp[:, :dsh].reshape(D, 3 * pw)
    vecs = allp[:, dsh : dsh + 6, :dsh].transpose(1, 0, 2).reshape(6, D).astype(F32)
    gains, biases = vecs[:2], vecs[2:]
    b_qv_full = (
        allp[:, dsh + 6, : b_qv.size]
        .reshape(n_sh, 2, heads, b_qv.shape[2])
        .transpose(1, 2, 0, 3)
        .reshape(2, pw)
        .astype(F32)
    )

    pad = ((0, R - frames), (0, 0))
    x_own = jnp.pad(frames_in[0], pad)
    g_own = jnp.pad(grad_out[0], pad)
    x_mlp = jnp.where(k == a, x_own, core_swap(x_own))
    g_mlp = jnp.where(k == a, g_own, core_swap(g_own))

    up_sh = jnp.concatenate([w_up, jnp.pad(b_up.reshape(1, -1), ((0, 15), (0, hid - b_up.size)))], axis=0)
    dn_sh = w_down.T

    def spread(x):
        near = perm_sz(x, lambda i, j: (i ^ 1, j ^ 2) if i % 2 == 0 else (i ^ 1, j))
        far = perm_sz(x, lambda i, j: (i, j) if i % 2 == 0 else (i, j ^ 2))
        cur = [far, near]
        for b in bits[1:]:
            cur = cur + [perm_s(y, lambda i: i ^ (1 << b)) for y in cur]
        stack = jnp.stack(cur)
        return jnp.concatenate([dyn(stack, s ^ i)[None] for i in range(n_sh)], axis=0)

    up_all = spread(up_sh)
    up_w = up_all[:, :dsh].reshape(D, hid)
    up_b = (
        up_all[:, dsh, : b_up.size]
        .reshape(n_sh, b_up.shape[0], b_up.shape[1])
        .transpose(1, 0, 2)
        .reshape(1, hid)
        .astype(F32)
    )
    dn_w = spread(dn_sh).reshape(D, hid)

    wo_sh = w_out.T
    cur = [jnp.stack([wo_sh] + [perm_z(wo_sh, lambda i, j=j: i ^ j) for j in (1, 2, 3)])]
    for b in bits:
        cur = cur + [perm_s(y, lambda i: i ^ (1 << b)) for y in cur]
    stack = jnp.stack(cur)
    wo_rows = jnp.concatenate([dyn(stack, s ^ i) for i in range(n_sh)], axis=1)

    xf = x_own.astype(F32)
    xh1, _ = norm_stats(xf)
    act_one = (xh1 * gains[0] + biases[0]).astype(BF)
    prod = dot(act_one, w_all, 1, 0)
    q = (prod[:, 2 * pw :] + b_qv_full[0]).astype(BF)
    kv_own, kv_oth = [], []
    for h in range(heads):
        bv = jnp.concatenate([jnp.zeros((hd,), F32), b_qv_full[1, h * hd : (h + 1) * hd]])
        kv = (prod[:, 2 * hd * h : 2 * hd * (h + 1)] + bv).astype(BF)
        kv_own.append(kv)
        kv_oth.append(perm_x(kv))

    first = tuple(range(heads - 1))
    last = heads - 1
    o_a, lse_a = attn_fwd(q, [(kv_own[h], kv_oth[h]) for h in first], first, hd, frames, scale)
    o_b, lse_b = attn_fwd(q, [(kv_own[last], kv_oth[last])], (last,), hd, frames, scale)
    o_b = jnp.concatenate([o_b[: R // 2], o_b[R // 2 :]], axis=1)

    def to_pair(x):
        one = perm_sz(x, lambda i, j: ((i & ~1) | (j & 1), 2 * (i & 1) + (j >> 1)))
        two = perm_sz(x, lambda i, j: ((i & ~1) | (j & 1), 2 * (i & 1) + 1 - (j >> 1)))
        return [one, core_swap(one), two, core_swap(two)]

    ra, rb = to_pair(o_a), to_pair(o_b)
    rb = [jnp.concatenate([y[:, :hd], y[:, hd:]], axis=0) for y in rb]
    obs = jnp.stack([jnp.concatenate([u, v], axis=1) for u, v in zip(ra, rb)])
    zs = 2 * p + k
    obs = [dyn(obs, zs ^ i) for i in range(4)]
    wos = [dyn(wo_rows, z ^ i) for i in range(4)]
    ob_cat = jnp.concatenate(obs, axis=1)
    wo_cat = jnp.concatenate(wos, axis=1)

    r1 = x_mlp.astype(F32) + (dot(ob_cat, wo_cat, 1, 1) + biases[1])
    xh2, rstd2 = norm_stats(r1)
    act_two = (xh2 * gains[1] + biases[2]).astype(BF)
    upper = dot(act_two, up_w, 1, 0) + up_b
    cdf = 0.5 * (1.0 + lax.erf(upper * ROOT_HALF))
    hb = (upper * cdf).astype(BF)
    mlp_part = dot(hb, dn_w, 1, 1).astype(BF)
    dhb = dot(g_mlp, dn_w, 1, 0)
    du = dhb * (cdf + upper * jnp.exp(-0.5 * upper * upper) * INV_ROOT_2PI)
    gu = du.astype(BF)
    dn2_part = dot(gu, up_w, 1, 1).astype(BF)

    def pair_sum(x):
        x = x.reshape(2, 2 * CH, D)
        y = dyn(x, k).astype(F32) + core_swap(dyn(x, 1 - k)).astype(F32)
        y = y.reshape(2, CH, D)
        return dyn(y, p) + perm_z(dyn(y, 1 - p).astype(BF), lambda i: i ^ 1).astype(F32)

    def own_rows(x):
        return lax.dynamic_slice_in_dim(x, o * CH, CH, 0)

    dn2 = pair_sum(dn2_part)
    r1_own, g_f = own_rows(r1), own_rows(g_mlp).astype(F32)
    xh2o, rstd2o = norm_stats(r1_own)
    dr1 = g_f + norm_back(dn2, gains[1], xh2o, rstd2o)
    ga = dr1.astype(BF)
    gob_own = [dot(ga, w, 1, 0).astype(BF) for w in wos]
    gob_own = jnp.stack(gob_own)

    def owner_to_clip(i, j, m):
        return ((i & ~1) | (j >> 1), (2 * (i & 1) + (j & 1)) ^ m)

    def clip_to_owner(i, j, m):
        r = j ^ m
        return ((i & ~1) | (r >> 1), 2 * (i & 1) + (r & 1))

    got = jnp.stack(
        [perm_sz(dyn(gob_own, o ^ m), lambda i, j, m=m: owner_to_clip(i, j, m)) for m in range(4)]
    )
    gob = jnp.concatenate([dyn(got, z ^ i) for i in range(4)], axis=0)

    lse = [lse_a[h : h + 1] for h in first] + [lse_b]
    dqs, dks, dvs = [], [], []
    for h in range(heads):
        dq, down, doth = attn_bwd(q, kv_own[h], kv_oth[h], lse[h], gob, h, hd, frames, scale)
        down = down + perm_x(doth).astype(F32)
        dqs.append(dq)
        dks.append(down[:, :hd])
        dvs.append(down[:, hd:])
    dq, dk, dv = (jnp.concatenate(t, axis=1) for t in (dqs, dks, dvs))
    sum_q, sum_v = jnp.sum(dq, axis=0), jnp.sum(dv, axis=0)
    gkv = []
    for h in range(heads):
        gkv += [dk[:, h * hd : (h + 1) * hd], dv[:, h * hd : (h + 1) * hd]]
    g_all = jnp.concatenate(gkv + [dq], axis=1).astype(BF)
    dn1_part = dot(g_all, w_all, 1, 1).astype(BF).reshape(4, CH, D)
    dn1 = sum(
        perm_sz(dyn(dn1_part, z ^ m), lambda i, j, m=m: clip_to_owner(i, j, m)).astype(F32)
        for m in range(4)
    )
    xh1o, rstd1o = norm_stats(own_rows(x_mlp).astype(F32))
    gin = dr1 + norm_back(dn1, gains[0], xh1o, rstd1o)

    def to_clip(x):
        y = jnp.stack([perm_sz(x, lambda i, j, m=m: owner_to_clip(i, j, m)) for m in range(4)])
        y = jnp.concatenate([dyn(y, z ^ i) for i in range(4)], axis=0)
        return y[:frames].astype(F32)[None]

    grad_in = to_clip(gin.astype(BF))
    mlp = pair_sum(mlp_part)
    block_out = to_clip((r1_own + (mlp + biases[3])).astype(BF))

    def halve(x, bit, send):
        mine, other = dyn(x, bit), dyn(x, 1 - bit)
        return (mine.astype(F32) + send(other).astype(F32)).astype(BF)

    def reduce_hi(x):
        for b in reversed(bits[1:]):
            y = x.reshape((2, x.shape[0] // 2) + x.shape[1:])
            x = halve(y, (s >> b) & 1, lambda t: perm_s(t, lambda i: i ^ (1 << b)))
        return x[0]

    g_up = dot(act_two, gu, 0, 0).astype(BF).reshape(n_sh // 2, 2, dsh, hid)
    g_dn = dot(g_mlp, hb, 0, 0).astype(BF).reshape(n_sh // 2, 2, dsh, hid)
    ff = reduce_hi(jnp.stack([g_up, g_dn], axis=2))
    ff = halve(ff, c, perm_x)
    ff = ff.astype(F32) + perm_sz(
        ff, lambda i, j: (i & ~1, j ^ 2) if i % 2 == 1 else None
    ).astype(F32)
    ff = ff.astype(BF)

    def perm_sx(x, f):
        pairs = []
        for i in range(n_sh):
            for j in range(2):
                t = f(i, j)
                if t is not None:
                    pairs.append((i * 2 + j, t[0] * 2 + t[1]))
        return lax.ppermute(x, ("shards", "context"), pairs)

    ff_one = perm_sx(ff, lambda i, j: None if i % 2 else (i | j, 1 - j))
    ff_two = perm_sx(ff, lambda i, j: None if i % 2 else (i | j, j))
    ff = jnp.where(c == k, ff_two, ff_one).astype(F32)
    grad_w_up, grad_w_down = ff[0], ff[1].T

    ob_rows = jnp.concatenate([own_rows(t) for t in obs], axis=1)
    g_wo = dot(ga, ob_rows, 0, 0).astype(BF)
    wo = halve(
        g_wo.reshape(n_sh // 2, 2, dsh, 4 * pw).transpose(1, 0, 2, 3), k, core_swap
    )
    wo = reduce_hi(wo)
    wo = jnp.stack([wo[:, i * pw : (i + 1) * pw] for i in range(4)])
    wo = dyn(wo, z).astype(F32) + sum(
        perm_z(dyn(wo, z ^ m), lambda i, m=m: i ^ m).astype(F32) for m in (1, 2, 3)
    )

    def over_x(x):
        x = x.astype(BF)
        return x.astype(F32) + perm_x(x).astype(F32)

    grad_w_out = over_x(wo).T

    wq_g = dot(act_one, g_all, 0, 0).astype(BF)
    wq_g = halve(wq_g.reshape(n_sh // 2, 2, dsh, 3 * pw).transpose(1, 0, 2, 3), k, core_swap)
    wq_g = over_x(reduce_hi(wq_g))
    gk = jnp.concatenate([wq_g[:, 2 * hd * h : 2 * hd * h + hd] for h in range(heads)], axis=1)
    gv = jnp.concatenate([wq_g[:, 2 * hd * h + hd : 2 * hd * (h + 1)] for h in range(heads)], axis=1)
    grad_w_qkv = jnp.stack([wq_g[:, 2 * pw :], gk, gv], axis=1)

    blk = jnp.where(k == 0, z, z ^ 2)
    row_sums = jnp.stack(
        [
            jnp.sum(dn1 * xh1o, axis=0),
            jnp.sum(dn2 * xh2o, axis=0),
            jnp.sum(dn1, axis=0),
            jnp.sum(dr1, axis=0),
            jnp.sum(dn2, axis=0),
            jnp.sum(g_f, axis=0),
        ]
    )
    up_slots = jnp.zeros((4, hid), F32)
    up_slots = lax.dynamic_update_index_in_dim(up_slots, jnp.sum(du, axis=0), blk, 0)
    qv_slots = jnp.zeros((4, 2 * pw), F32)
    qv_slots = lax.dynamic_update_index_in_dim(qv_slots, jnp.concatenate([sum_q, sum_v]), z, 0)
    vec = jnp.concatenate([row_sums.reshape(-1), up_slots.reshape(-1), qv_slots.reshape(-1)])
    vec = vec.reshape(-1, 128)
    for b in bits:
        vec = vec + perm_s(vec, lambda i: i ^ (1 << b))
    vec = vec + perm_x(vec)
    for b in (1, 2):
        vec = vec + perm_z(vec, lambda i: i ^ b)
    vec = vec.reshape(-1)
    n0 = 6 * D
    n1 = n0 + 4 * hid
    rows6 = lax.dynamic_slice_in_dim(vec[:n0].reshape(6, D), s * dsh, dsh, 1)
    upb = dyn(vec[n0:n1].reshape(4, b_up.shape[0], hd), z)
    grad_b_up = lax.dynamic_slice_in_dim(upb, s * b_up.shape[1], b_up.shape[1], 1)
    qvb = dyn(vec[n1:].reshape(4, 2, heads, hd), z)
    grad_b_qv = lax.dynamic_slice_in_dim(qvb, s * b_qv.shape[2], b_qv.shape[2], 2)
    return (
        block_out,
        grad_in,
        rows6[:2],
        rows6[2:],
        grad_w_qkv,
        grad_b_qv,
        grad_w_out,
        grad_w_up,
        grad_b_up,
        grad_w_down,
    )


def solution(mesh):
    placed = (
        P("shards", "context", None),
        P("shards", "context", None),
        P(None, "shards"),
        P(None, "shards"),
        P("shards", None, "tensor"),
        P(None, "tensor", "shards"),
        P("tensor", "shards"),
        P("shards", "tensor"),
        P("tensor", "shards"),
        P("tensor", "shards"),
    )
    return jax.shard_map(
        per_device,
        mesh=mesh,
        in_specs=placed,
        out_specs=placed[:4] + placed[4:],
        check_vma=False,
    )
```
